32 devices in a mesh: row: 4 (over z), col: 8 (over y, x, core).
Axes of the slice: x: 2, y: 2, z: 4, core: 2. Of those that a mesh axis runs over, the one named last changes fastest.
Arguments:
- charges: bfloat16 [64, 48, 1024], P(('row', 'col')), may hold values from -6 to 6
- near_blocks: bfloat16 [64, 2, 1024, 1024], P(('row', 'col')), may hold values from -0.125 to 0.125
- near_src: int32 [64, 2], P(('row', 'col')), may hold values from 0 to 63, as said below
- far_v: bfloat16 [32, 32, 4, 32, 1024], P(('row', 'col')), may hold values from -0.1875 to 0.1875
- far_u: bfloat16 [32, 32, 4, 32, 1024], P(('row', 'col')), may hold values from -0.125 to 0.125
- far_rank: int32 [32, 32, 4], P(('row', 'col')), may hold values from 0 to 32, as said below
- far_col: int32 [32, 32, 4], P(('row', 'col')), may hold values from 0 to 1
- far_row: int32 [32, 32, 4], P(('row', 'col')), may hold values from 0 to 1
Outputs:
- potential: float32 [64, 48, 1024], P(('row', 'col'))
The draws below stay inside these ranges and needn't reach their ends.
Inputs may be any that keep to these rules, and one draw needn't show every extreme that they name: near_src[i, n] is a cluster of a device with the same row index as cluster i's device, whose col index differs from it by at most one, cyclically over 8. `far_rank`: in every draw some device receives only used slots (rank above 0) from every device.
All inputs are finite; a program needn't handle non-finite values.
Results may differ from the reference program's by a relative error of at most 0.0017.
Values may be sent and summed in bfloat16 or wider, within the bound.
A program may use at most 128 MiB of HBM per device.

```python
import jax
import jax.numpy as jnp
from jax import lax

M = 1024
R = 32
RHS = 48
NEAR = 2
FAR_IN = 128
CL_DEV = 2
CLUSTERS = 64
CAP = 4
N_ROW = 4
N_COL = 8
DEVICES = 32


def draw_near_src(key, part):
    first, second = jax.random.split(jax.random.fold_in(key, 11))
    cluster = jnp.arange(CLUSTERS, dtype=jnp.int32)[:, None]
    device = cluster // CL_DEV
    row_index = device // N_COL
    col_index = device % N_COL
    offset = jax.random.randint(first, (CLUSTERS, NEAR), -1, 2)
    within = jax.random.randint(second, (CLUSTERS, NEAR), 0, CL_DEV)
    target = (row_index * N_COL + (col_index + offset + N_COL) % N_COL) * CL_DEV + within
    return target.astype(jnp.int32)


def draw_far_rank(key, part):
    first, second, third = jax.random.split(jax.random.fold_in(key, 23), 3)
    shape = (DEVICES, DEVICES, CAP)
    live = jax.random.randint(first, shape, 0, 10) < 7
    chosen = jax.random.randint(third, (), 0, DEVICES)
    filled = jnp.arange(DEVICES, dtype=jnp.int32)[None, :, None] == chosen
    ranks = jax.random.randint(second, shape, R // 4, R + 1)
    return jnp.where(live | filled, ranks, 0).astype(jnp.int32)


def plant(drawn, stream_key, least, high):
    longest = drawn.shape.index(max(drawn.shape))
    spots = []
    for shift in (0, 1):
        where = [jax.random.randint(jax.random.fold_in(stream_key, axis), (), 0, length) for axis, length in enumerate(drawn.shape)]
        where[longest] = (where[longest] + shift) % drawn.shape[longest]
        spots.append(tuple(where))
    return drawn.at[spots[0]].set(least).at[spots[1]].set(high)


def steps_of(own_key, shape, pieces, smallest, high):
    loudness, own = 1.0, jax.random.fold_in(own_key, 6)
    for dim, parts in pieces:
        steps = jnp.exp(jax.random.uniform(jax.random.fold_in(own, dim), (parts,), jnp.float32, smallest / len(pieces), high / len(pieces)))
        loudness = loudness * jnp.repeat(steps, shape[dim] // parts).reshape([-1 if axis == dim else 1 for axis in range(len(shape))])
    return loudness


def centred(key, dims, scale, reach, pieces=(), held_as=jnp.bfloat16):
    entries = jax.random.normal(key, dims, jnp.float32) * scale
    if len(pieces) > 0:
        entries = steps_of(key, dims, pieces, -0.22, 0.18) * entries
    return jnp.clip(entries, min=-reach, max=reach).astype(held_as)


def setup_inputs(seed: int = 0) -> dict:
    key_list = jax.random.split(jax.random.key(seed), 9)
    charges = centred(key_list[0], (CLUSTERS, RHS, M), 1.0, 6.0, ((0, 32),))
    near_blocks = centred(key_list[1], (CLUSTERS, NEAR, M, M), (NEAR * M) ** -0.5, 0.125, ((0, 32),))
    near_src = draw_near_src(jax.random.fold_in(key_list[8], 71), 0)
    far_v = centred(key_list[3], (DEVICES, DEVICES, CAP, R, M), M ** -0.5, 0.1875, ((0, 32),))
    far_u = centred(key_list[4], (DEVICES, DEVICES, CAP, R, M), (R * FAR_IN // 2) ** -0.5, 0.125, ((0, 32),))
    far_rank = draw_far_rank(jax.random.fold_in(key_list[8], 71), 0)
    far_col = plant(jax.random.randint(key_list[6], (DEVICES, DEVICES, CAP), 0, CL_DEV), jax.random.fold_in(key_list[6], 1), 0, CL_DEV - 1).astype(jnp.int32)
    far_row = plant(jax.random.randint(key_list[7], (DEVICES, DEVICES, CAP), 0, CL_DEV), jax.random.fold_in(key_list[7], 1), 0, CL_DEV - 1).astype(jnp.int32)
    return {"charges": charges, "near_blocks": near_blocks, "near_src": near_src, "far_v": far_v, "far_u": far_u, "far_rank": far_rank, "far_col": far_col, "far_row": far_row}


def reference(charges, near_blocks, near_src, far_v, far_u, far_rank, far_col, far_row):
    devices = N_ROW * N_COL
    width = far_v.shape[3]

    def near_one(item):
        blocks, sources = item
        picked = charges[sources].astype(jnp.float32)
        return jnp.einsum("nsa,nab->sb", picked, blocks.astype(jnp.float32))

    near = lax.map(near_one, (near_blocks, near_src))
    grouped = charges.reshape(devices, CL_DEV, charges.shape[1], charges.shape[2])
    columns = jnp.arange(width, dtype=jnp.int32)

    def send_one(item):
        mine, factors, ranks, picks = item
        selected = mine[picks].astype(jnp.float32)
        proj = jnp.einsum("ecsm,ecrm->ecsr", selected, factors.astype(jnp.float32))
        keep = (columns[None, None, :] < ranks[:, :, None]).astype(jnp.float32)
        return (proj * keep[:, :, None, :]).astype(jnp.bfloat16)

    coef = lax.map(send_one, (grouped, far_v, far_rank, far_col))
    coef_t = jnp.swapaxes(coef, 0, 1)
    locals_ = jnp.arange(CL_DEV, dtype=jnp.int32)

    def receive_one(item):
        incoming, factors, rows = item
        onehot = (rows[:, :, None] == locals_[None, None, :]).astype(jnp.float32)
        spread = incoming.astype(jnp.float32)[:, :, None, :, :] * onehot[:, :, :, None, None]
        return jnp.einsum("dclsr,dcrm->lsm", spread, factors.astype(jnp.float32))

    far = lax.map(receive_one, (coef_t, far_u, far_row))
    far = far.reshape(charges.shape)
    return near + far
```

```python
import functools

import jax
import jax.numpy as jnp
from jax import lax
from jax.experimental import pallas as pl
from jax.experimental.pallas import tpu as pltpu
from jax.sharding import PartitionSpec as P

MESH = pl.DeviceIdType.MESH
CHUNK_LANES = 512


def kernel(
    rows, cols, group,
    nsrc, ch_hbm, nb_hbm, fv_hbm, fu_hbm, rank_hbm, col_hbm, row_hbm,
    out,
    src, nb, fv, fu, small, spread, send, recv,
    src_sem, nb_sem, fv_sem, fu_sem, small_sem, halo_send, halo_recv, far_send, far_recv,
):
    devices = rows * cols
    clusters, rhs, elements = src.shape[1:]
    slots, width = fv_hbm.shape[2:4]
    lanes = slots * width
    chunks = devices // group
    row_here, col_here = lax.axis_index("row"), lax.axis_index("col")
    me = row_here * cols + col_here
    chunk_here = me // group

    def place(device):
        return (device // cols, device % cols)

    own_copy = pltpu.make_async_copy(ch_hbm, src.at[1], src_sem)
    own_copy.start()
    small_copies = [
        pltpu.make_async_copy(ref, small.at[pl.ds(i, 1)], small_sem.at[i])
        for i, ref in enumerate((rank_hbm, col_hbm, row_hbm))
    ]
    for copy in small_copies:
        copy.start()

    def fv_copy(g):
        chunk = (chunk_here + g) % chunks
        return pltpu.make_async_copy(fv_hbm.at[0, pl.ds(chunk * group, group)], fv.at[g], fv_sem.at[g])

    def fu_copy(g):
        chunk = (chunk_here - g + chunks) % chunks
        return pltpu.make_async_copy(fu_hbm.at[0, pl.ds(chunk * group, group)], fu.at[g], fu_sem.at[g])

    def nb_copy(l, n):
        return pltpu.make_async_copy(nb_hbm.at[l, n], nb.at[l, n], nb_sem.at[l, n])

    near = nb_hbm.shape[1]
    for g in range(chunks):
        fv_copy(g).start()

    barrier = pltpu.get_barrier_semaphore()

    @pl.loop(1, devices)
    def _(step):
        pl.semaphore_signal(barrier, inc=1, device_id=place((me + step) % devices), device_id_type=MESH)

    for l in range(clusters):
        for n in range(near):
            nb_copy(l, n).start()
    for g in range(chunks):
        fu_copy(g).start()

    for copy in small_copies:
        copy.wait()
    for i in range(3):
        table = small[i]
        tall = [jnp.broadcast_to(table[c : c + 1], (width, devices)) for c in range(slots)]
        spread[i] = jnp.concatenate(tall, axis=0).T

    own_copy.wait()
    right = (row_here, (col_here + 1) % cols)
    left = (row_here, (col_here + cols - 1) % cols)
    halos = [
        pltpu.make_async_remote_copy(
            src.at[1], src.at[slot], halo_send.at[i], halo_recv.at[i], device_id=where, device_id_type=MESH
        )
        for i, (slot, where) in enumerate(((0, right), (2, left)))
    ]
    column = lax.broadcasted_iota(jnp.int32, (1, lanes), 1) % width

    def project(g):
        fv_copy(g).wait()
        chunk = (chunk_here + g) % chunks
        mine = src[1].reshape(clusters * rhs, elements)
        factors = fv[g].reshape(group * lanes, elements)
        proj = lax.dot_general(mine, factors, (((1,), (1,)), ((), ())), preferred_element_type=jnp.float32)
        for j in range(group):
            e = chunk * group + j
            part = proj[:, j * lanes : (j + 1) * lanes]
            pick = spread[1, pl.ds(e, 1), :]
            chosen = part[:rhs]
            for l in range(1, clusters):
                chosen = jnp.where(pick == l, part[l * rhs : (l + 1) * rhs], chosen)
            keep = column < spread[0, pl.ds(e, 1), :]
            send[e] = jnp.where(keep, chosen, 0.0).astype(jnp.bfloat16)

    def far_copy(e, source):
        return pltpu.make_async_remote_copy(
            send.at[e], recv.at[source], far_send.at[e], far_recv.at[source], device_id=place(e), device_id_type=MESH
        )

    def post(g):
        chunk = (chunk_here + g) % chunks

        @pl.loop(0, group)
        def _(j):
            e = chunk * group + j

            @pl.when(e != me)
            def _():
                far_copy(e, me).start()

    project(0)
    pl.semaphore_wait(barrier, devices - 1)
    for copy in halos:
        copy.start()

    @pl.loop(1, chunks)
    def _(g):
        project(g)
        post(g - 1)

    recv[me] = send[me]
    out[...] = jnp.zeros_like(out)
    post(chunks - 1)

    for copy in halos:
        copy.wait_recv()
    for l in range(clusters):
        for n in range(near):
            index = nsrc[l, n]
            source_col = index // clusters % cols
            slot = jnp.minimum((source_col - col_here + 1 + cols) % cols, 2)
            picked = src[slot, index % clusters]
            nb_copy(l, n).wait()
            out[l] += jnp.dot(picked, nb[l, n], preferred_element_type=jnp.float32)

    @pl.loop(0, chunks)
    def _(g):
        chunk = (chunk_here - g + chunks) % chunks

        @pl.loop(0, group)
        def _(j):
            d = chunk * group + j

            @pl.when(d != me)
            def _():
                far_copy(d, d).wait_recv()

        fu_copy(g).wait()
        parts = [[] for _ in range(clusters)]
        for j in range(group):
            d = chunk * group + j
            incoming = recv[d].astype(jnp.float32)
            target = spread[2, pl.ds(d, 1), :]
            for l in range(clusters):
                parts[l].append(jnp.where(target == l, incoming, 0.0).astype(jnp.bfloat16))
        left_side = jnp.concatenate([jnp.concatenate(p, axis=1) for p in parts], axis=0)
        factors = fu[g].reshape(group * lanes, elements)
        product = jnp.dot(left_side, factors, preferred_element_type=jnp.float32)
        out[...] += product.reshape(out.shape)

    for copy in halos:
        copy.wait_send()

    @pl.loop(1, devices)
    def _(step):
        far_copy((me + step) % devices, me).wait_send()


def local(charges, near_blocks, near_src, far_v, far_u, far_rank, far_col, far_row):
    cols = lax.axis_size("col")
    rows = lax.axis_size("row")
    devices = rows * cols
    clusters, rhs, elements = charges.shape
    near = near_blocks.shape[1]
    slots, width = far_v.shape[2:4]
    lanes = slots * width
    group = max(1, min(devices, CHUNK_LANES // lanes))
    while devices % group:
        group -= 1
    chunks = devices // group
    anywhere = pl.BlockSpec(memory_space=pl.ANY)
    factors = (chunks, group, slots, width, elements)
    tables = [jnp.swapaxes(table, 1, 2) for table in (far_rank, far_col, far_row)]
    return pl.pallas_call(
        functools.partial(kernel, rows, cols, group),
        out_shape=pltpu.VMEM((clusters, rhs, elements), jnp.float32),
        in_specs=[pl.BlockSpec(memory_space=pltpu.SMEM)] + [anywhere] * 7,
        out_specs=pl.BlockSpec(memory_space=pltpu.VMEM),
        scratch_shapes=[
            pltpu.VMEM((3, clusters, rhs, elements), jnp.bfloat16),
            pltpu.VMEM(near_blocks.shape, jnp.bfloat16),
            pltpu.VMEM(factors, jnp.bfloat16),
            pltpu.VMEM(factors, jnp.bfloat16),
            pltpu.VMEM((3, slots, devices), jnp.int32),
            pltpu.VMEM((3, devices, lanes), jnp.int32),
            pltpu.VMEM((devices, rhs, lanes), jnp.bfloat16),
            pltpu.VMEM((devices, rhs, lanes), jnp.bfloat16),
            pltpu.SemaphoreType.DMA,
            pltpu.SemaphoreType.DMA((clusters, near)),
            pltpu.SemaphoreType.DMA((chunks,)),
            pltpu.SemaphoreType.DMA((chunks,)),
            pltpu.SemaphoreType.DMA((3,)),
            pltpu.SemaphoreType.DMA((2,)),
            pltpu.SemaphoreType.DMA((2,)),
            pltpu.SemaphoreType.DMA((devices,)),
            pltpu.SemaphoreType.DMA((devices,)),
        ],
        compiler_params=pltpu.CompilerParams(
            collective_id=0, has_side_effects=True, vmem_limit_bytes=60 * 1024 * 1024
        ),
    )(near_src, charges, near_blocks, far_v, far_u, *tables)


def solution(mesh):
    return jax.shard_map(
        local,
        mesh=mesh,
        in_specs=(
            P(("row", "col"), None, None),
            P(("row", "col"), None, None, None),
            P(("row", "col"), None),
            P(("row", "col"), None, None, None, None),
            P(("row", "col"), None, None, None, None),
            P(("row", "col"), None, None),
            P(("row", "col"), None, None),
            P(("row", "col"), None, None),
        ),
        out_specs=P(("row", "col"), None, None),
        check_vma=False,
    )
```

```python
import functools

import jax
import jax.numpy as jnp
from jax import lax
from jax.experimental import pallas as pl
from jax.experimental.pallas import tpu as pltpu
from jax.sharding import PartitionSpec as P

MESH = pl.DeviceIdType.MESH
CHUNK_LANES = 512


def kernel(
    rows, cols, group,
    nsrc, ch_hbm, nb_hbm, fv_hbm, fu_hbm, rank_hbm, col_hbm, row_hbm,
    out,
    src, nb, fv, fu, small, spread, send, recv,
    src_sem, nb_sem, fv_sem, fu_sem, small_sem, halo_send, halo_recv, far_send, far_recv,
):
    devices = rows * cols
    clusters, rhs, elements = src.shape[1:]
    slots, width = fv_hbm.shape[2:4]
    lanes = slots * width
    chunks = devices // group
    row_here, col_here = lax.axis_index("row"), lax.axis_index("col")
    me = row_here * cols + col_here
    chunk_here = me // group

    def place(device):
        return (device // cols, device % cols)

    own_copy = pltpu.make_async_copy(ch_hbm, src.at[1], src_sem)
    own_copy.start()
    small_copies = [
        pltpu.make_async_copy(ref, small.at[pl.ds(i, 1)], small_sem.at[i])
        for i, ref in enumerate((rank_hbm, col_hbm, row_hbm))
    ]
    for copy in small_copies:
        copy.start()

    def fv_copy(g):
        chunk = (chunk_here + g) % chunks
        return pltpu.make_async_copy(fv_hbm.at[0, pl.ds(chunk * group, group)], fv.at[g], fv_sem.at[g])

    def fu_copy(g):
        chunk = (chunk_here - g + chunks) % chunks
        return pltpu.make_async_copy(fu_hbm.at[0, pl.ds(chunk * group, group)], fu.at[g], fu_sem.at[g])

    def nb_copy(l, n):
        return pltpu.make_async_copy(nb_hbm.at[l, n], nb.at[l, n], nb_sem.at[l, n])

    near = nb_hbm.shape[1]
    for g in range(chunks):
        fv_copy(g).start()

    barrier = pltpu.get_barrier_semaphore()

    @pl.loop(1, devices)
    def _(step):
        pl.semaphore_signal(barrier, inc=1, device_id=place((me + step) % devices), device_id_type=MESH)

    for l in range(clusters):
        for n in range(near):
            nb_copy(l, n).start()
    for g in range(chunks):
        fu_copy(g).start()

    for copy in small_copies:
        copy.wait()
    for i in range(3):
        table = small[i]
        tall = [jnp.broadcast_to(table[c : c + 1], (width, devices)) for c in range(slots)]
        spread[i] = jnp.concatenate(tall, axis=0).T

    own_copy.wait()
    right = (row_here, (col_here + 1) % cols)
    left = (row_here, (col_here + cols - 1) % cols)
    halos = [
        pltpu.make_async_remote_copy(
            src.at[1], src.at[slot], halo_send.at[i], halo_recv.at[i], device_id=where, device_id_type=MESH
        )
        for i, (slot, where) in enumerate(((0, right), (2, left)))
    ]
    column = lax.broadcasted_iota(jnp.int32, (1, lanes), 1) % width

    def project(g):
        fv_copy(g).wait()
        chunk = (chunk_here + g) % chunks
        mine = src[1].reshape(clusters * rhs, elements)
        factors = fv[g].reshape(group * lanes, elements)
        proj = lax.dot_general(mine, factors, (((1,), (1,)), ((), ())), preferred_element_type=jnp.float32)
        for j in range(group):
            e = chunk * group + j
            part = proj[:, j * lanes : (j + 1) * lanes]
            pick = spread[1, pl.ds(e, 1), :]
            chosen = part[:rhs]
            for l in range(1, clusters):
                chosen = jnp.where(pick == l, part[l * rhs : (l + 1) * rhs], chosen)
            keep = column < spread[0, pl.ds(e, 1), :]
            send[e] = jnp.where(keep, chosen, 0.0).astype(jnp.bfloat16)

    def far_copy(e, source):
        return pltpu.make_async_remote_copy(
            send.at[e], recv.at[source], far_send.at[e], far_recv.at[source], device_id=place(e), device_id_type=MESH
        )

    def post(g):
        chunk = (chunk_here + g) % chunks

        @pl.loop(0, group)
        def _(j):
            e = chunk * group + j

            @pl.when(e != me)
            def _():
                far_copy(e, me).start()

    project(0)
    pl.semaphore_wait(barrier, devices - 1)
    for copy in halos:
        copy.start()

    @pl.loop(1, chunks)
    def _(g):
        project(g)
        post(g - 1)

    recv[me] = send[me]
    out[...] = jnp.zeros_like(out)
    post(chunks - 1)

    for copy in halos:
        copy.wait_recv()
    for l in range(clusters):
        for n in range(near):
            index = nsrc[l, n]
            source_col = index // clusters % cols
            slot = jnp.minimum((source_col - col_here + 1 + cols) % cols, 2)
            picked = src[slot, index % clusters]
            nb_copy(l, n).wait()
            out[l] += jnp.dot(picked, nb[l, n], preferred_element_type=jnp.float32)

    @pl.loop(0, chunks, unroll=True)
    def _(g):
        chunk = (chunk_here - g + chunks) % chunks

        @pl.loop(0, group)
        def _(j):
            d = chunk * group + j

            @pl.when(d != me)
            def _():
                far_copy(d, d).wait_recv()

        fu_copy(g).wait()
        parts = [[] for _ in range(clusters)]
        for j in range(group):
            d = chunk * group + j
            incoming = recv[d].astype(jnp.float32)
            target = spread[2, pl.ds(d, 1), :]
            for l in range(clusters):
                parts[l].append(jnp.where(target == l, incoming, 0.0).astype(jnp.bfloat16))
        left_side = jnp.concatenate([jnp.concatenate(p, axis=1) for p in parts], axis=0)
        factors = fu[g].reshape(group * lanes, elements)
        product = jnp.dot(left_side, factors, preferred_element_type=jnp.float32)
        out[...] += product.reshape(out.shape)

    for copy in halos:
        copy.wait_send()

    @pl.loop(1, devices)
    def _(step):
        far_copy((me + step) % devices, me).wait_send()


def local(charges, near_blocks, near_src, far_v, far_u, far_rank, far_col, far_row):
    cols = lax.axis_size("col")
    rows = lax.axis_size("row")
    devices = rows * cols
    clusters, rhs, elements = charges.shape
    near = near_blocks.shape[1]
    slots, width = far_v.shape[2:4]
    lanes = slots * width
    group = max(1, min(devices, CHUNK_LANES // lanes))
    while devices % group:
        group -= 1
    chunks = devices // group
    anywhere = pl.BlockSpec(memory_space=pl.ANY)
    factors = (chunks, group, slots, width, elements)
    tables = [jnp.swapaxes(table, 1, 2) for table in (far_rank, far_col, far_row)]
    return pl.pallas_call(
        functools.partial(kernel, rows, cols, group),
        out_shape=pltpu.VMEM((clusters, rhs, elements), jnp.float32),
        in_specs=[pl.BlockSpec(memory_space=pltpu.SMEM)] + [anywhere] * 7,
        out_specs=pl.BlockSpec(memory_space=pltpu.VMEM),
        scratch_shapes=[
            pltpu.VMEM((3, clusters, rhs, elements), jnp.bfloat16),
            pltpu.VMEM(near_blocks.shape, jnp.bfloat16),
            pltpu.VMEM(factors, jnp.bfloat16),
            pltpu.VMEM(factors, jnp.bfloat16),
            pltpu.VMEM((3, slots, devices), jnp.int32),
            pltpu.VMEM((3, devices, lanes), jnp.int32),
            pltpu.VMEM((devices, rhs, lanes), jnp.bfloat16),
            pltpu.VMEM((devices, rhs, lanes), jnp.bfloat16),
            pltpu.SemaphoreType.DMA,
            pltpu.SemaphoreType.DMA((clusters, near)),
            pltpu.SemaphoreType.DMA((chunks,)),
            pltpu.SemaphoreType.DMA((chunks,)),
            pltpu.SemaphoreType.DMA((3,)),
            pltpu.SemaphoreType.DMA((2,)),
            pltpu.SemaphoreType.DMA((2,)),
            pltpu.SemaphoreType.DMA((devices,)),
            pltpu.SemaphoreType.DMA((devices,)),
        ],
        compiler_params=pltpu.CompilerParams(
            collective_id=0, has_side_effects=True, vmem_limit_bytes=60 * 1024 * 1024
        ),
    )(near_src, charges, near_blocks, far_v, far_u, *tables)


def solution(mesh):
    return jax.shard_map(
        local,
        mesh=mesh,
        in_specs=(
            P(("row", "col"), None, None),
            P(("row", "col"), None, None, None),
            P(("row", "col"), None),
            P(("row", "col"), None, None, None, None),
            P(("row", "col"), None, None, None, None),
            P(("row", "col"), None, None),
            P(("row", "col"), None, None),
            P(("row", "col"), None, None),
        ),
        out_specs=P(("row", "col"), None, None),
        check_vma=False,
    )
```
